32 devices in a mesh: dp: 4 (over z), adapter: 2 (over x), fsdp: 4 (over y, core).
Axes of the slice: x: 2, y: 2, z: 4, core: 2. Of those that a mesh axis runs over, the one named last changes fastest.
Arguments:
- adapter_index: int32 [768], P(('dp', 'adapter', 'fsdp')), may hold values from 0 to 1, as said below
- output_gradient: bfloat16 [768, 4096], P(('dp', 'adapter', 'fsdp')), may hold values from -6 to 6
- hidden: bfloat16 [768, 14336], P(('dp', 'adapter', 'fsdp')), may hold values from -6 to 6
- frozen_down_weight: bfloat16 [14336, 4096], P('adapter', 'fsdp'), may hold values from -0.046875 to 0.046875
- adapter_input_maps: bfloat16 [2, 16, 14336], P('adapter'), may hold values from -0.046875 to 0.046875
- adapter_output_maps: bfloat16 [2, 16, 4096], P('adapter'), may hold values from -1.5 to 1.5
Outputs:
- hidden_gradient: bfloat16 [768, 14336], P(('dp', 'adapter', 'fsdp'))
- adapter_input_gradient: float32 [2, 16, 14336], P('adapter')
- adapter_output_gradient: float32 [2, 16, 4096], P('adapter')
The draws below stay inside these ranges and needn't reach their ends.
Inputs may be any that keep to these rules, and one draw needn't show every extreme that they name: `adapter_index`: adapter i sits at index i // 1 of adapter. Of the 24 tokens of one device (aligned blocks of 24 rows), at most 12 name adapters at the same index; in every draw one index is named by exactly 12 tokens of every device.
All inputs are finite; a program needn't handle non-finite values.
Results may differ from the reference program's by a relative error of at most 0.015.
Values may be sent and summed in bfloat16 or wider, within the bound.
A program may use at most 64 MiB of HBM per device.

```python
import jax
import jax.numpy as jnp
from jax import lax

MODEL_DIM = 4096
FEED_HIDDEN = 14336
ADAPTER_RANK = 16
TOK_DEV = 24
ADP_DEV = 1
CAP = 12
ADAPTER_COUNT = 2
TOKEN_COUNT = 768
N_FSDP = 4


def draw_adapter_index(key, part):
    block_total = TOKEN_COUNT // TOK_DEV
    owner_total = ADAPTER_COUNT // ADP_DEV
    key_hot, key_slots, key_rows, key_local = jax.random.split(key, 4)
    hot_owner = jax.random.randint(key_hot, (), 0, owner_total).astype(jnp.int32)
    slot_total = (owner_total - 1) * CAP
    slot_owner = jnp.arange(slot_total, dtype=jnp.int32) // CAP
    slot_owner = slot_owner + (slot_owner >= hot_owner).astype(jnp.int32)
    scores = jax.random.randint(key_slots, (block_total, slot_total), 0, 1 << 20) * slot_total + jnp.arange(slot_total, dtype=jnp.int32)[None, :]
    ordering = jnp.argsort(scores, axis=1, stable=True)
    picked = slot_owner[ordering[:, :TOK_DEV - CAP]]
    row_owner = jnp.concatenate([jnp.full((block_total, CAP), hot_owner, dtype=jnp.int32), picked.astype(jnp.int32)], axis=1)
    shuffle_keys = jax.random.randint(key_rows, (block_total, TOK_DEV), 0, 1 << 20) * TOK_DEV + jnp.arange(TOK_DEV, dtype=jnp.int32)[None, :]
    shuffled = jnp.argsort(shuffle_keys, axis=1, stable=True)
    row_owner = jnp.take_along_axis(row_owner, shuffled, axis=1)
    local_pick = jax.random.randint(key_local, (block_total, TOK_DEV), 0, ADP_DEV).astype(jnp.int32)
    return (row_owner * ADP_DEV + local_pick).reshape(TOKEN_COUNT).astype(jnp.int32)


def shard_levels(stream_key, dims, pieces, least, largest):
    gain = 1.0
    for axis_at, shards_of in pieces:
        heights = jax.random.uniform(jax.random.fold_in(jax.random.fold_in(stream_key, 6), axis_at), (shards_of,), jnp.float32, least / len(pieces), largest / len(pieces))
        gain = gain * jnp.repeat(jnp.exp(heights), dims[axis_at] // shards_of).reshape((-1,) + (1,) * (len(dims) - 1 - axis_at))
    return gain


def noise(stream_key, dims, width, bound, shards=(), kind=jnp.bfloat16):
    entries = width * jax.random.normal(stream_key, dims, jnp.float32)
    if shards:
        entries = entries * shard_levels(stream_key, dims, shards, -0.22, 0.18)
    return jnp.clip(entries, -bound, bound).astype(kind)


def setup_inputs(seed: int = 0) -> dict:
    seeds = jax.random.split(jax.random.key(seed), 7)
    return {
        "adapter_index": draw_adapter_index(jax.random.fold_in(seeds[6], 71), 0),
        "output_gradient": noise(seeds[1], (TOKEN_COUNT, MODEL_DIM), 1.0, 6.0, ((0, 32),)),
        "hidden": noise(seeds[2], (TOKEN_COUNT, FEED_HIDDEN), 1.0, 6.0, ((0, 32),)),
        "frozen_down_weight": noise(seeds[3], (FEED_HIDDEN, MODEL_DIM), FEED_HIDDEN ** -0.5, 0.046875, ((0, 2), (1, 4))),
        "adapter_input_maps": noise(seeds[4], (ADAPTER_COUNT, ADAPTER_RANK, FEED_HIDDEN), FEED_HIDDEN ** -0.5, 0.046875, ((0, 2),)),
        "adapter_output_maps": noise(seeds[5], (ADAPTER_COUNT, ADAPTER_RANK, MODEL_DIM), ADAPTER_RANK ** -0.5, 1.5, ((0, 2),)),
    }


adapter_scale = 2.0


def reference(adapter_index, output_gradient, hidden, frozen_down_weight, adapter_input_maps, adapter_output_maps):
    flattened_input_map = adapter_input_maps.reshape(ADAPTER_COUNT * ADAPTER_RANK, FEED_HIDDEN)
    flattened_output_map = adapter_output_maps.reshape(ADAPTER_COUNT * ADAPTER_RANK, MODEL_DIM)
    selected = adapter_index.astype(jnp.int32)[:, None] == jnp.arange(ADAPTER_COUNT).astype(jnp.int32)[None, :]
    token_mask = jnp.repeat(selected, ADAPTER_RANK, axis=1).astype(jnp.float32)
    slab_width = MODEL_DIM // N_FSDP
    base_total = jnp.zeros((TOKEN_COUNT, FEED_HIDDEN), jnp.float32)
    for block_index in range(N_FSDP):
        lhs_cols = output_gradient[:, block_index * slab_width:(block_index + 1) * slab_width]
        rhs_cols = frozen_down_weight[:, block_index * slab_width:(block_index + 1) * slab_width]
        block_part = lax.dot_general(lhs_cols, rhs_cols, (((1,), (1,)), ((), ())), preferred_element_type=jnp.float32).astype(jnp.bfloat16)
        block_part = lax.optimization_barrier(block_part)
        base_total = base_total + block_part.astype(jnp.float32)
    frozen_term = base_total.astype(jnp.bfloat16)
    multiplier = (lax.dot_general(output_gradient, flattened_output_map, (((1,), (1,)), ((), ())), preferred_element_type=jnp.float32) * token_mask).astype(jnp.bfloat16)
    low_rank = (lax.dot_general(hidden, flattened_input_map, (((1,), (1,)), ((), ())), preferred_element_type=jnp.float32) * token_mask).astype(jnp.bfloat16)
    adapter_term = (adapter_scale * jnp.dot(multiplier, flattened_input_map, preferred_element_type=jnp.float32)).astype(jnp.bfloat16)
    hidden_gradient = (frozen_term.astype(jnp.float32) + adapter_term.astype(jnp.float32)).astype(jnp.bfloat16)
    scaling_factor = adapter_scale * ADAPTER_COUNT / TOKEN_COUNT
    input_map_gradient = lax.dot_general(multiplier, hidden, (((0,), (0,)), ((), ())), preferred_element_type=jnp.float32)
    output_map_gradient = lax.dot_general(low_rank, output_gradient, (((0,), (0,)), ((), ())), preferred_element_type=jnp.float32)
    adapter_input_gradient = (scaling_factor * input_map_gradient).reshape(ADAPTER_COUNT, ADAPTER_RANK, FEED_HIDDEN)
    adapter_output_gradient = (scaling_factor * output_map_gradient).reshape(ADAPTER_COUNT, ADAPTER_RANK, MODEL_DIM)
    return (hidden_gradient, adapter_input_gradient, adapter_output_gradient)
```

```python
import functools

import jax
import jax.numpy as jnp
from jax import lax
from jax.experimental import pallas as pl
from jax.experimental.pallas import tpu as pltpu
from jax.sharding import PartitionSpec as P

adapter_scale = 2.0


def on_device(
    adapter_index,
    output_gradient,
    hidden,
    frozen_down_weight,
    adapter_input_maps,
    adapter_output_maps,
):
    tok_rows = output_gradient.shape[0]
    token_tenants = lax.axis_size("adapter")
    fibres = lax.axis_size("fsdp")
    groups = lax.axis_size("dp")
    tenant_token_count = adapter_input_maps.shape[0]
    adapter_rank_size = adapter_input_maps.shape[1]
    hidden_units_width = hidden.shape[1]
    model_dimension_width = output_gradient.shape[1]
    capacity = max(2, min(tok_rows // 2, 2 * tok_rows // token_tenants))
    every_token = tok_rows * token_tenants * fibres * groups
    scaling_factor = adapter_scale * (tenant_token_count * token_tenants) / every_token
    slab_width = frozen_down_weight.shape[1]
    own_columns = lax.all_to_all(output_gradient, "fsdp", split_axis=1, concat_axis=0, tiled=True)
    spread = lax.all_gather(own_columns, "adapter", axis=0, tiled=True)
    blocks = spread.reshape(token_tenants, fibres, tok_rows, slab_width)
    per_fibre = token_tenants * tok_rows
    taken = blocks
    taken = jnp.transpose(taken, (1, 0, 2, 3)).reshape(
        per_fibre * lax.axis_size("fsdp"), slab_width
    )
    partial_base = lax.psum_scatter(
        lax.dot_general(
            taken, frozen_down_weight, (((1,), (1,)), ((), ())), preferred_element_type=jnp.float32
        ).astype(jnp.bfloat16),
        "fsdp",
        scatter_dimension=0,
        tiled=True,
    )
    frozen_term = lax.all_to_all(partial_base, "adapter", split_axis=0, concat_axis=1, tiled=True)
    owner_of = adapter_index // tenant_token_count
    local_of = adapter_index - owner_of * tenant_token_count
    same_owner = owner_of[:, None] == owner_of[None, :]
    earlier = jnp.arange(tok_rows)[None, :] < jnp.arange(tok_rows)[:, None]
    position = jnp.sum((same_owner & earlier).astype(jnp.int32), axis=1)
    slot_of = owner_of * capacity + position
    slot_count = token_tenants * capacity
    placing = (jnp.arange(slot_count, dtype=jnp.int32)[:, None] == slot_of[None, :]).astype(
        jnp.bfloat16
    )
    send_out = jnp.dot(placing, output_gradient, preferred_element_type=jnp.float32).astype(
        jnp.bfloat16
    )
    send_hidden = jnp.dot(placing, hidden, preferred_element_type=jnp.float32).astype(jnp.bfloat16)
    send_tag = jnp.dot(
        placing, (local_of + 1).astype(jnp.bfloat16), preferred_element_type=jnp.float32
    ).astype(jnp.bfloat16)
    recv_out, recv_hidden, recv_tag = (
        lax.all_to_all(send_out, "adapter", split_axis=0, concat_axis=0, tiled=True),
        lax.all_to_all(send_hidden, "adapter", split_axis=0, concat_axis=0, tiled=True),
        lax.all_to_all(send_tag, "adapter", split_axis=0, concat_axis=0, tiled=True),
    )
    flattened_input_map = adapter_input_maps.reshape(
        tenant_token_count * adapter_rank_size, hidden_units_width
    )
    flattened_output_map = adapter_output_maps.reshape(
        tenant_token_count * adapter_rank_size, model_dimension_width
    )
    chosen = (
        recv_tag.astype(jnp.float32)[:, None]
        == (jnp.arange(tenant_token_count) + 1).astype(jnp.float32)[None, :]
    )
    row_mask = jnp.repeat(chosen, adapter_rank_size, axis=1).astype(jnp.float32)
    multiplier = (
        lax.dot_general(
            recv_out,
            flattened_output_map,
            (((1,), (1,)), ((), ())),
            preferred_element_type=jnp.float32,
        )
        * row_mask
    ).astype(jnp.bfloat16)
    low_rank = (
        lax.dot_general(
            recv_hidden,
            flattened_input_map,
            (((1,), (1,)), ((), ())),
            preferred_element_type=jnp.float32,
        )
        * row_mask
    ).astype(jnp.bfloat16)
    adapter_token_rows = (
        adapter_scale * jnp.dot(multiplier, flattened_input_map, preferred_element_type=jnp.float32)
    ).astype(jnp.bfloat16)
    grad_a_part = lax.dot_general(
        multiplier, recv_hidden, (((0,), (0,)), ((), ())), preferred_element_type=jnp.float32
    )
    grad_b_part = lax.dot_general(
        low_rank, recv_out, (((0,), (0,)), ((), ())), preferred_element_type=jnp.float32
    )
    backward_result = lax.all_to_all(
        adapter_token_rows, "adapter", split_axis=0, concat_axis=0, tiled=True
    )
    adapter_selection = lax.dot_general(
        placing, backward_result, (((0,), (0,)), ((), ())), preferred_element_type=jnp.float32
    )
    hidden_gradient = (frozen_term.astype(jnp.float32) + adapter_selection).astype(jnp.bfloat16)
    input_map_total, output_map_total = (
        lax.psum(grad_a_part.astype(jnp.bfloat16), ("dp", "fsdp")).astype(jnp.float32),
        lax.psum(grad_b_part.astype(jnp.bfloat16), ("dp", "fsdp")).astype(jnp.float32),
    )
    adapter_input_gradient = (scaling_factor * input_map_total).reshape(
        tenant_token_count, adapter_rank_size, hidden_units_width
    )
    adapter_output_gradient = (scaling_factor * output_map_total).reshape(
        tenant_token_count, adapter_rank_size, model_dimension_width
    )
    return (hidden_gradient, adapter_input_gradient, adapter_output_gradient)


def chunk_count(width):
    for count in (7, 8, 4, 2):
        if width % (count * 128) == 0:
            return count
    return 1


def fused_kernel(
    scale, chunks, idx_ref, og_ref, hid_ref, w_ref, a_ref, b_ref,
    out_ref, ga_ref, gb_ref,
    wv, xrec, xs, keep, psend, prec, ysend, yrec, xsend, xrecv,
    aoth, both,
    gsend_a, gkeep_a, grec_a, zs_a, zrec_a, sum_a, xg_a, xgrec_a, yg_a, ygrec_a, full_a,
    gsend_b, gkeep_b, grec_b, zs_b, zrec_b, sum_b, xg_b, xgrec_b, yg_b, ygrec_b, full_b,
    wsem, ssem, rsem, csend, crecv,
):
    f32, bf16 = jnp.float32, jnp.bfloat16
    d, a, f = lax.axis_index("dp"), lax.axis_index("adapter"), lax.axis_index("fsdp")
    groups = lax.axis_size("dp")
    c = lax.rem(f, 2)
    y = f // 2
    toks = og_ref.shape[0]
    half = w_ref.shape[0]
    slab = w_ref.shape[1]
    ch = half // chunks
    hidden_width = hid_ref.shape[1]
    model_width = og_ref.shape[1]
    fc = 2 * y + (1 - c)
    fy = 2 * (1 - y) + c
    core, ynb, xnb = (d, a, fc), (d, a, fy), (d, 1 - a, f)

    def plane(yr, cr, ar):
        yy = (1 - y) if yr else y
        cc = (1 - c) if cr else c
        return (d, (1 - a) if ar else a, 2 * yy + cc)

    peers = [(yr, cr, ar) for yr in (1, 0) for cr in (0, 1) for ar in (0, 1) if yr or cr or ar]

    def zdev(r):
        return (lax.rem(d + r, groups), a, f)

    counter = [0]

    def remote(src, dst, dev):
        k = counter[0]
        counter[0] += 1
        return pltpu.make_async_remote_copy(
            src_ref=src, dst_ref=dst, send_sem=ssem.at[k], recv_sem=rsem.at[k],
            device_id=dev, device_id_type=pl.DeviceIdType.MESH,
        )

    started = []

    def go(copy):
        copy.start()
        started.append(copy)
        return copy

    def cols(start, width, align):
        return pl.ds(pl.multiple_of(start, align), width)

    def w_copy(j):
        return pltpu.make_async_copy(
            w_ref.at[pl.ds(pl.multiple_of(j * ch, ch), ch), :], wv.at[j], wsem.at[j]
        )

    for j in range(chunks):
        w_copy(j).start()

    barrier = pltpu.get_barrier_semaphore()
    all_peers = [plane(*p) for p in peers] + [zdev(r) for r in range(1, groups)]
    for dev in all_peers:
        pl.semaphore_signal(barrier, inc=1, device_id=dev, device_id_type=pl.DeviceIdType.MESH)
    pl.semaphore_wait(barrier, len(all_peers))

    hb = model_width // 2
    ha = hidden_width // 2
    bcols = cols(c * hb, hb, hb)
    acols = cols(c * ha, ha, ha)
    bx = go(remote(b_ref.at[0, :, bcols], both.at[:, bcols], xnb))
    ogc = []
    for p in peers:
        dev = plane(*p)
        ogc.append(
            go(remote(og_ref.at[:, cols(dev[2] * slab, slab, slab)], xrec.at[p[0], p[1], p[2]], dev))
        )
    ax = go(remote(a_ref.at[0, :, acols], aoth.at[:, acols], xnb))
    bx.wait_recv()
    bp = go(remote(both.at[:, bcols], both.at[:, bcols], core))

    def nt(lhs, rhs):
        return lax.dot_general(lhs, rhs, (((1,), (1,)), ((), ())), preferred_element_type=f32)

    own_mask = (idx_ref[...] == a).astype(f32)
    oth_mask = (idx_ref[...] == 1 - a).astype(f32)

    def masked_pair(lhs, own, oth):
        return jnp.concatenate(
            [nt(lhs, own) * own_mask, nt(lhs, oth) * oth_mask], axis=1
        )

    def grad_first(left_t, ref, gsend, gkeep, grec, width):
        gsend[...] = jnp.dot(
            left_t, ref[:, cols((1 - c) * width, width, width)], preferred_element_type=f32
        ).astype(bf16)
        copy = go(remote(gsend, grec, core))
        gkeep[...] = jnp.dot(
            left_t, ref[:, cols(c * width, width, width)], preferred_element_type=f32
        )
        return copy

    def grad_z(copy, gkeep, grec, zs, zrec):
        copy.wait_recv()
        wq = zs.shape[2]
        for q in range(groups):
            zs[q] = (
                gkeep[:, q * wq : (q + 1) * wq] + grec[:, q * wq : (q + 1) * wq].astype(f32)
            ).astype(bf16)
        return [
            go(remote(zs.at[lax.rem(d + r, groups)], zrec.at[r - 1], zdev(r)))
            for r in range(1, groups)
        ]

    def grad_x(copies, zs, zrec, acc, xg, xgrec):
        for copy in copies:
            copy.wait_recv()
        total = zs[d].astype(f32)
        for r in range(groups - 1):
            total = total + zrec[r].astype(f32)
        rank = total.shape[0] // 2
        acc[...] = total[:rank]
        xg[...] = total[rank:].astype(bf16)
        return go(remote(xg, xgrec, xnb))

    def grad_y(copy, acc, xgrec, yg, ygrec):
        copy.wait_recv()
        yg[...] = (acc[...] + xgrec[...].astype(f32)).astype(bf16)
        return go(remote(yg, ygrec, ynb))

    def grad_gather(copy, yg, ygrec, full):
        copy.wait_recv()
        full[c, d] = (yg[...].astype(f32) + ygrec[...].astype(f32)).astype(bf16)
        return [
            go(remote(full.at[c, d], full.at[c, d], zdev(r))) for r in range(1, groups)
        ]

    def grad_core(copies, full):
        for copy in copies:
            copy.wait_recv()
        return go(remote(full.at[c], full.at[c], core))

    def grad_out(copy, full, ref):
        copy.wait_recv()
        wq = full.shape[3]
        for h in range(2):
            for q in range(groups):
                at = (h * groups + q) * wq
                ref[0, :, at : at + wq] = scale * full[h, q].astype(f32)

    bp.wait_recv()
    og = og_ref[...]
    coef = masked_pair(og, b_ref[0], both[...])
    coef_t = jnp.transpose(coef, (1, 0)).astype(bf16)
    rank = coef.shape[1] // 2
    coef_own = coef[:, :rank].astype(bf16)
    coef_oth = coef[:, rank:].astype(bf16)
    ga1 = grad_first(coef_t, hid_ref, gsend_a, gkeep_a, grec_a, ha)

    for copy in ogc:
        copy.wait_recv()
    at = 0
    for yr in (0, 1):
        for cr in (0, 1):
            rows = []
            for ar in (0, 1):
                if yr or cr or ar:
                    rows.append(xrec[yr, cr, ar].astype(f32))
                else:
                    rows.append(og_ref[:, cols(f * slab, slab, slab)].astype(f32))
            pair = jnp.concatenate(rows, axis=0).astype(bf16)
            xs[at : at + 2 * toks] = pair
            at += 2 * toks

    def chunk_copy(k, src, dst, dev, j):
        return pltpu.make_async_remote_copy(
            src_ref=src.at[j], dst_ref=dst.at[j], send_sem=csend.at[k, j],
            recv_sem=crecv.at[k, j], device_id=dev, device_id_type=pl.DeviceIdType.MESH,
        )

    def core_copy(j):
        return chunk_copy(0, psend, prec, core, j)

    def y_copy(j):
        return chunk_copy(1, ysend, yrec, ynb, j)

    def x_copy(j):
        return chunk_copy(2, xsend, xrecv, xnb, j)

    pair_rows = 2 * toks

    def stage_matmul(j):
        w_copy(j).wait()
        part = nt(xs[...], wv[j])
        for yr in (0, 1):
            at = 2 * yr * pair_rows
            keep[j, yr] = part[at : at + pair_rows]
            psend[j, yr] = part[at + pair_rows : at + 2 * pair_rows].astype(bf16)
        core_copy(j).start()

    def stage_y(j):
        core_copy(j).wait_recv()
        ysend[j] = (keep[j, 1] + prec[j, 1].astype(f32)).astype(bf16)
        y_copy(j).start()

    def lora(at):
        own = jnp.dot(coef_own, a_ref[0, :, at], preferred_element_type=f32)
        oth = jnp.dot(coef_oth, aoth[:, at], preferred_element_type=f32)
        return (adapter_scale * (own + oth)).astype(bf16).astype(f32)

    def stage_x(j):
        y_copy(j).wait_recv()
        total = keep[j, 0] + prec[j, 0].astype(f32) + yrec[j].astype(f32)
        xsend[j] = total[toks:].astype(bf16)
        x_copy(j).start()
        at = cols(a * half + j * ch, ch, ch)
        own = total[:toks].astype(bf16).astype(f32)
        out_ref[:, at] = (own + lora(at)).astype(bf16)

    def stage_out(j):
        x_copy(j).wait_recv()
        at = cols((1 - a) * half + j * ch, ch, ch)
        out_ref[:, at] = (xrecv[j].astype(f32) + lora(at)).astype(bf16)

    def loop(first, last):
        @pl.loop(first, last)
        def _(j):
            stage_matmul(j)
            stage_y(j - 1)

    mid = min(chunks, 1 + chunks // 2)
    stage_matmul(0)
    loop(1, mid)
    ga2 = grad_z(ga1, gkeep_a, grec_a, zs_a, zrec_a)
    ax.wait_recv()
    ap = go(remote(aoth.at[:, acols], aoth.at[:, acols], core))
    loop(mid, chunks)
    stage_y(chunks - 1)
    ap.wait_recv()
    low = masked_pair(hid_ref[...], a_ref[0], aoth[...])
    low_t = jnp.transpose(low, (1, 0)).astype(bf16)
    gb1 = grad_first(low_t, og_ref, gsend_b, gkeep_b, grec_b, hb)

    state = {}

    def s_gb2():
        state["gb2"] = grad_z(gb1, gkeep_b, grec_b, zs_b, zrec_b)

    def s_ga3():
        state["ga3"] = grad_x(ga2, zs_a, zrec_a, sum_a, xg_a, xgrec_a)

    def s_ga4():
        state["ga4"] = grad_y(state["ga3"], sum_a, xgrec_a, yg_a, ygrec_a)

    def s_gb3():
        state["gb3"] = grad_x(state["gb2"], zs_b, zrec_b, sum_b, xg_b, xgrec_b)

    def s_ga5():
        state["ga5"] = grad_gather(state["ga4"], yg_a, ygrec_a, full_a)

    def s_gb4():
        state["gb4"] = grad_y(state["gb3"], sum_b, xgrec_b, yg_b, ygrec_b)

    def s_gb5():
        state["gb5"] = grad_gather(state["gb4"], yg_b, ygrec_b, full_b)

    def s_ga6():
        state["ga6"] = grad_core(state["ga5"], full_a)

    def s_gb6():
        state["gb6"] = grad_core(state["gb5"], full_b)

    between = [[s_gb2], [s_ga3], [s_ga4, s_gb3], [s_gb4, s_ga5], [s_gb5], [s_ga6], [s_gb6]]
    for j in range(max(chunks, len(between))):
        if j < chunks:
            stage_x(j)
        if j < len(between):
            for step in between[j]:
                step()
    for j in range(chunks):
        stage_out(j)
    grad_out(state["ga6"], full_a, ga_ref)
    grad_out(state["gb6"], full_b, gb_ref)
    for copy in started:
        copy.wait_send()
    for j in range(chunks):
        core_copy(j).wait_send()
        y_copy(j).wait_send()
        x_copy(j).wait_send()


def fused_on_device(
    adapter_index, output_gradient, hidden, frozen_down_weight, adapter_input_maps,
    adapter_output_maps,
):
    toks, model_width = output_gradient.shape
    hidden_width = hidden.shape[1]
    half, slab = frozen_down_weight.shape
    rank = adapter_input_maps.shape[1]
    groups = lax.axis_size("dp")
    devices = groups * lax.axis_size("adapter") * lax.axis_size("fsdp")
    scale = adapter_scale * lax.axis_size("adapter") / (toks * devices)
    chunks = chunk_count(half)
    ch = half // chunks
    f32, bf16 = jnp.float32, jnp.bfloat16

    def grad_scratch(width):
        wh = width // 2
        wq = wh // groups
        return [
            pltpu.VMEM((2 * rank, wh), bf16),
            pltpu.VMEM((2 * rank, wh), f32),
            pltpu.VMEM((2 * rank, wh), bf16),
            pltpu.VMEM((groups, 2 * rank, wq), bf16),
            pltpu.VMEM((groups - 1, 2 * rank, wq), bf16),
            pltpu.VMEM((rank, wq), f32),
            pltpu.VMEM((rank, wq), bf16),
            pltpu.VMEM((rank, wq), bf16),
            pltpu.VMEM((rank, wq), bf16),
            pltpu.VMEM((rank, wq), bf16),
            pltpu.VMEM((2, groups, rank, wq), bf16),
        ]

    copies = 4 + 7 + 2 * (4 + 2 * (groups - 1))
    vmem = pl.BlockSpec(memory_space=pltpu.VMEM)
    return pl.pallas_call(
        functools.partial(fused_kernel, scale, chunks),
        out_shape=(
            jax.ShapeDtypeStruct((toks, hidden_width), bf16),
            jax.ShapeDtypeStruct((1, rank, hidden_width), f32),
            jax.ShapeDtypeStruct((1, rank, model_width), f32),
        ),
        in_specs=[vmem, vmem, vmem, pl.BlockSpec(memory_space=pl.ANY), vmem, vmem],
        out_specs=(vmem, vmem, vmem),
        scratch_shapes=[
            pltpu.VMEM((chunks, ch, slab), bf16),
            pltpu.VMEM((2, 2, 2, toks, slab), bf16),
            pltpu.VMEM((8 * toks, slab), bf16),
            pltpu.VMEM((chunks, 2, 2 * toks, ch), f32),
            pltpu.VMEM((chunks, 2, 2 * toks, ch), bf16),
            pltpu.VMEM((chunks, 2, 2 * toks, ch), bf16),
            pltpu.VMEM((chunks, 2 * toks, ch), bf16),
            pltpu.VMEM((chunks, 2 * toks, ch), bf16),
            pltpu.VMEM((chunks, toks, ch), bf16),
            pltpu.VMEM((chunks, toks, ch), bf16),
            pltpu.VMEM((rank, hidden_width), bf16),
            pltpu.VMEM((rank, model_width), bf16),
            *grad_scratch(hidden_width),
            *grad_scratch(model_width),
            pltpu.SemaphoreType.DMA((chunks,)),
            pltpu.SemaphoreType.DMA((copies,)),
            pltpu.SemaphoreType.DMA((copies,)),
            pltpu.SemaphoreType.DMA((3, chunks)),
            pltpu.SemaphoreType.DMA((3, chunks)),
        ],
        compiler_params=pltpu.CompilerParams(collective_id=0, has_side_effects=True),
    )(
        adapter_index.reshape(toks, 1), output_gradient, hidden, frozen_down_weight,
        adapter_input_maps, adapter_output_maps,
    )


def per_device(mesh):
    def body(*args):
        fused = (
            mesh.shape["adapter"] == 2
            and mesh.shape["fsdp"] == 4
            and args[4].shape[0] == 1
        )
        return fused_on_device(*args) if fused else on_device(*args)

    return body


def solution(mesh):
    in_specs = (
        P(("dp", "adapter", "fsdp")),
        P(("dp", "adapter", "fsdp"), None),
        P(("dp", "adapter", "fsdp"), None),
        P("adapter", "fsdp"),
        P("adapter", None, None),
        P("adapter", None, None),
    )
    out_specs = (
        P(("dp", "adapter", "fsdp"), None),
        P("adapter", None, None),
        P("adapter", None, None),
    )
    return jax.shard_map(
        per_device(mesh), mesh=mesh, in_specs=in_specs, out_specs=out_specs, check_vma=False
    )
```

```python
import functools

import jax
import jax.numpy as jnp
from jax import lax
from jax.experimental import pallas as pl
from jax.experimental.pallas import tpu as pltpu
from jax.sharding import PartitionSpec as P

adapter_scale = 2.0


def on_device(
    adapter_index,
    output_gradient,
    hidden,
    frozen_down_weight,
    adapter_input_maps,
    adapter_output_maps,
):
    tok_rows = output_gradient.shape[0]
    token_tenants = lax.axis_size("adapter")
    fibres = lax.axis_size("fsdp")
    groups = lax.axis_size("dp")
    tenant_token_count = adapter_input_maps.shape[0]
    adapter_rank_size = adapter_input_maps.shape[1]
    hidden_units_width = hidden.shape[1]
    model_dimension_width = output_gradient.shape[1]
    capacity = max(2, min(tok_rows // 2, 2 * tok_rows // token_tenants))
    every_token = tok_rows * token_tenants * fibres * groups
    scaling_factor = adapter_scale * (tenant_token_count * token_tenants) / every_token
    slab_width = frozen_down_weight.shape[1]
    own_columns = lax.all_to_all(output_gradient, "fsdp", split_axis=1, concat_axis=0, tiled=True)
    spread = lax.all_gather(own_columns, "adapter", axis=0, tiled=True)
    blocks = spread.reshape(token_tenants, fibres, tok_rows, slab_width)
    per_fibre = token_tenants * tok_rows
    taken = blocks
    taken = jnp.transpose(taken, (1, 0, 2, 3)).reshape(
        per_fibre * lax.axis_size("fsdp"), slab_width
    )
    partial_base = lax.psum_scatter(
        lax.dot_general(
            taken, frozen_down_weight, (((1,), (1,)), ((), ())), preferred_element_type=jnp.float32
        ).astype(jnp.bfloat16),
        "fsdp",
        scatter_dimension=0,
        tiled=True,
    )
    frozen_term = lax.all_to_all(partial_base, "adapter", split_axis=0, concat_axis=1, tiled=True)
    owner_of = adapter_index // tenant_token_count
    local_of = adapter_index - owner_of * tenant_token_count
    same_owner = owner_of[:, None] == owner_of[None, :]
    earlier = jnp.arange(tok_rows)[None, :] < jnp.arange(tok_rows)[:, None]
    position = jnp.sum((same_owner & earlier).astype(jnp.int32), axis=1)
    slot_of = owner_of * capacity + position
    slot_count = token_tenants * capacity
    placing = (jnp.arange(slot_count, dtype=jnp.int32)[:, None] == slot_of[None, :]).astype(
        jnp.bfloat16
    )
    send_out = jnp.dot(placing, output_gradient, preferred_element_type=jnp.float32).astype(
        jnp.bfloat16
    )
    send_hidden = jnp.dot(placing, hidden, preferred_element_type=jnp.float32).astype(jnp.bfloat16)
    send_tag = jnp.dot(
        placing, (local_of + 1).astype(jnp.bfloat16), preferred_element_type=jnp.float32
    ).astype(jnp.bfloat16)
    recv_out, recv_hidden, recv_tag = (
        lax.all_to_all(send_out, "adapter", split_axis=0, concat_axis=0, tiled=True),
        lax.all_to_all(send_hidden, "adapter", split_axis=0, concat_axis=0, tiled=True),
        lax.all_to_all(send_tag, "adapter", split_axis=0, concat_axis=0, tiled=True),
    )
    flattened_input_map = adapter_input_maps.reshape(
        tenant_token_count * adapter_rank_size, hidden_units_width
    )
    flattened_output_map = adapter_output_maps.reshape(
        tenant_token_count * adapter_rank_size, model_dimension_width
    )
    chosen = (
        recv_tag.astype(jnp.float32)[:, None]
        == (jnp.arange(tenant_token_count) + 1).astype(jnp.float32)[None, :]
    )
    row_mask = jnp.repeat(chosen, adapter_rank_size, axis=1).astype(jnp.float32)
    multiplier = (
        lax.dot_general(
            recv_out,
            flattened_output_map,
            (((1,), (1,)), ((), ())),
            preferred_element_type=jnp.float32,
        )
        * row_mask
    ).astype(jnp.bfloat16)
    low_rank = (
        lax.dot_general(
            recv_hidden,
            flattened_input_map,
            (((1,), (1,)), ((), ())),
            preferred_element_type=jnp.float32,
        )
        * row_mask
    ).astype(jnp.bfloat16)
    adapter_token_rows = (
        adapter_scale * jnp.dot(multiplier, flattened_input_map, preferred_element_type=jnp.float32)
    ).astype(jnp.bfloat16)
    grad_a_part = lax.dot_general(
        multiplier, recv_hidden, (((0,), (0,)), ((), ())), preferred_element_type=jnp.float32
    )
    grad_b_part = lax.dot_general(
        low_rank, recv_out, (((0,), (0,)), ((), ())), preferred_element_type=jnp.float32
    )
    backward_result = lax.all_to_all(
        adapter_token_rows, "adapter", split_axis=0, concat_axis=0, tiled=True
    )
    adapter_selection = lax.dot_general(
        placing, backward_result, (((0,), (0,)), ((), ())), preferred_element_type=jnp.float32
    )
    hidden_gradient = (frozen_term.astype(jnp.float32) + adapter_selection).astype(jnp.bfloat16)
    input_map_total, output_map_total = (
        lax.psum(grad_a_part.astype(jnp.bfloat16), ("dp", "fsdp")).astype(jnp.float32),
        lax.psum(grad_b_part.astype(jnp.bfloat16), ("dp", "fsdp")).astype(jnp.float32),
    )
    adapter_input_gradient = (scaling_factor * input_map_total).reshape(
        tenant_token_count, adapter_rank_size, hidden_units_width
    )
    adapter_output_gradient = (scaling_factor * output_map_total).reshape(
        tenant_token_count, adapter_rank_size, model_dimension_width
    )
    return (hidden_gradient, adapter_input_gradient, adapter_output_gradient)


def chunk_count(width):
    for count in (7, 8, 4, 2):
        if width % (count * 128) == 0:
            return count
    return 1


def fused_kernel(
    chunks, idx_ref, og_hbm, hid_hbm, w_ref, a_hbm, b_hbm,
    out_ref, ga_ref, gb_ref,
    og_ref, hid_ref, a_ref, b_ref, wv, xrec, xs, keep, psend, prec, ysend, yrec, xsend, xrecv,
    aoth, both,
    gsend_a, gkeep_a, grec_a, zs_a, zrec_a, sum_a, xg_a, xgrec_a, yg_a, ygrec_a, full_a,
    gsend_b, gkeep_b, grec_b, zs_b, zrec_b, sum_b, xg_b, xgrec_b, yg_b, ygrec_b, full_b,
    lsem, wsem, ssem, rsem, csend, crecv,
):
    f32, bf16 = jnp.float32, jnp.bfloat16
    d, a, f = lax.axis_index("dp"), lax.axis_index("adapter"), lax.axis_index("fsdp")
    groups = lax.axis_size("dp")
    c = lax.rem(f, 2)
    y = f // 2
    toks = og_ref.shape[0]
    half = w_ref.shape[0]
    slab = w_ref.shape[1]
    ch = half // chunks
    hidden_width = hid_ref.shape[1]
    model_width = og_ref.shape[1]
    fc = 2 * y + (1 - c)
    fy = 2 * (1 - y) + c
    core, ynb, xnb = (d, a, fc), (d, a, fy), (d, 1 - a, f)

    def plane(yr, cr, ar):
        yy = (1 - y) if yr else y
        cc = (1 - c) if cr else c
        return (d, (1 - a) if ar else a, 2 * yy + cc)

    peers = [(yr, cr, ar) for yr in (1, 0) for cr in (0, 1) for ar in (0, 1) if yr or cr or ar]

    def zdev(r):
        return (lax.rem(d + r, groups), a, f)

    counter = [0]

    def remote(src, dst, dev):
        k = counter[0]
        counter[0] += 1
        return pltpu.make_async_remote_copy(
            src_ref=src, dst_ref=dst, send_sem=ssem.at[k], recv_sem=rsem.at[k],
            device_id=dev, device_id_type=pl.DeviceIdType.MESH,
        )

    started = []

    def go(copy):
        copy.start()
        started.append(copy)
        return copy

    def cols(start, width, align):
        return pl.ds(pl.multiple_of(start, align), width)

    def w_copy(j):
        return pltpu.make_async_copy(
            w_ref.at[pl.ds(pl.multiple_of(j * ch, ch), ch), :], wv.at[j], wsem.at[j]
        )

    local = [
        pltpu.make_async_copy(src, dst, lsem.at[k])
        for k, (src, dst) in enumerate(
            ((og_hbm, og_ref), (b_hbm, b_ref), (hid_hbm, hid_ref), (a_hbm, a_ref))
        )
    ]
    local[0].start()
    w_copy(0).start()
    w_copy(1).start()
    for copy in local[1:]:
        copy.start()
    for j in range(2, chunks):
        w_copy(j).start()

    barrier = pltpu.get_barrier_semaphore()
    all_peers = [plane(*p) for p in peers] + [zdev(r) for r in range(1, groups)]
    for dev in all_peers:
        pl.semaphore_signal(barrier, inc=1, device_id=dev, device_id_type=pl.DeviceIdType.MESH)
    pl.semaphore_wait(barrier, len(all_peers))

    hb = model_width // 2
    ha = hidden_width // 2
    bcols = cols(c * hb, hb, hb)
    acols = cols(c * ha, ha, ha)
    bx = go(remote(b_hbm.at[0, :, bcols], both.at[:, bcols], xnb))
    ogc = []
    for p in peers:
        dev = plane(*p)
        ogc.append(
            go(remote(og_hbm.at[:, cols(dev[2] * slab, slab, slab)], xrec.at[p[0], p[1], p[2]], dev))
        )
    ax = go(remote(a_hbm.at[0, :, acols], aoth.at[:, acols], xnb))

    def nt(lhs, rhs):
        return lax.dot_general(lhs, rhs, (((1,), (1,)), ((), ())), preferred_element_type=f32)

    own_mask = (idx_ref[...] == a).astype(f32)
    oth_mask = (idx_ref[...] == 1 - a).astype(f32)

    def masked_pair(own, oth, rhs):
        return jnp.concatenate([nt(own, rhs) * own_mask, nt(oth, rhs) * oth_mask], axis=0)

    def grad_first(left_t, ref, gsend, gkeep, grec, width):
        gsend[...] = jnp.dot(
            left_t, ref[:, cols((1 - c) * width, width, width)], preferred_element_type=f32
        ).astype(bf16)
        copy = go(remote(gsend, grec, core))
        gkeep[...] = jnp.dot(
            left_t, ref[:, cols(c * width, width, width)], preferred_element_type=f32
        )
        return copy

    def grad_z(copy, gkeep, grec, zs, zrec):
        copy.wait_recv()
        wq = zs.shape[2]
        for q in range(groups):
            zs[q] = (
                gkeep[:, q * wq : (q + 1) * wq] + grec[:, q * wq : (q + 1) * wq].astype(f32)
            ).astype(bf16)
        return [
            go(remote(zs.at[lax.rem(d + r, groups)], zrec.at[r - 1], zdev(r)))
            for r in range(1, groups)
        ]

    def grad_x(copies, zs, zrec, acc, xg, xgrec):
        for copy in copies:
            copy.wait_recv()
        total = zs[d].astype(f32)
        for r in range(groups - 1):
            total = total + zrec[r].astype(f32)
        rank = total.shape[0] // 2
        acc[...] = total[:rank]
        xg[...] = total[rank:].astype(bf16)
        return go(remote(xg, xgrec, xnb))

    def grad_y(copy, acc, xgrec, yg, ygrec):
        copy.wait_recv()
        yg[...] = (acc[...] + xgrec[...].astype(f32)).astype(bf16)
        return go(remote(yg, ygrec, ynb))

    def grad_gather(copy, yg, ygrec, full):
        copy.wait_recv()
        full[c, d] = (yg[...].astype(f32) + ygrec[...].astype(f32)).astype(bf16)
        out = [
            go(remote(full.at[c, d], full.at[c, d], zdev(r))) for r in range(1, groups)
        ]
        return out, [go(remote(full.at[c, d], full.at[c, d], core))]

    def grad_core(state, full):
        copies, sent = state
        for r, copy in enumerate(copies, 1):
            copy.wait_recv()
            at = lax.rem(d + groups - r, groups)
            sent.append(go(remote(full.at[c, at], full.at[c, at], core)))
        return sent

    def grad_out(copies, full, ref):
        for copy in copies:
            copy.wait_recv()
        ref[...] = full[...]

    def chunk_copy(k, src, dst, dev, j):
        return pltpu.make_async_remote_copy(
            src_ref=src.at[j], dst_ref=dst.at[j], send_sem=csend.at[k, j],
            recv_sem=crecv.at[k, j], device_id=dev, device_id_type=pl.DeviceIdType.MESH,
        )

    def core_copy(j):
        return chunk_copy(0, psend, prec, core, j)

    def y_copy(j):
        return chunk_copy(1, ysend, yrec, ynb, j)

    def x_copy(j):
        return chunk_copy(2, xsend, xrecv, xnb, j)

    pair_rows = 2 * toks

    def stage_matmul(j):
        w_copy(j).wait()
        part = nt(xs[...], wv[j])
        for yr in (0, 1):
            at = 2 * yr * pair_rows
            keep[j, yr] = part[at : at + pair_rows]
            psend[j, yr] = part[at + pair_rows : at + 2 * pair_rows].astype(bf16)
        core_copy(j).start()

    def stage_y(j):
        core_copy(j).wait_recv()
        ysend[j] = (keep[j, 1] + prec[j, 1].astype(f32)).astype(bf16)
        y_copy(j).start()

    def lora(at):
        coef_own, coef_oth = state["coef"]
        own = jnp.dot(coef_own, a_ref[0, :, at], preferred_element_type=f32)
        oth = jnp.dot(coef_oth, aoth[:, at], preferred_element_type=f32)
        return (adapter_scale * (own + oth)).astype(bf16).astype(f32)

    def stage_x(j):
        y_copy(j).wait_recv()
        total = keep[j, 0] + prec[j, 0].astype(f32) + yrec[j].astype(f32)
        xsend[j] = total[toks:].astype(bf16)
        x_copy(j).start()
        at = cols(a * half + j * ch, ch, ch)
        own = total[:toks].astype(bf16).astype(f32)
        out_ref[:, at] = (own + lora(at)).astype(bf16)

    def stage_out(j):
        x_copy(j).wait_recv()
        at = cols((1 - a) * half + j * ch, ch, ch)
        out_ref[:, at] = (xrecv[j].astype(f32) + lora(at)).astype(bf16)

    state = {}

    def s_b():
        bx.wait_recv()
        state["bp"] = go(remote(both.at[:, bcols], both.at[:, bcols], core))

    def s_coef():
        for copy in local[:3]:
            copy.wait()
        state["bp"].wait_recv()
        coef_t = masked_pair(b_ref[0], both[...], og_ref[...])
        coef = jnp.transpose(coef_t, (1, 0)).astype(bf16)
        rank = coef.shape[1] // 2
        state["coef"] = (coef[:, :rank], coef[:, rank:])
        state["ga1"] = grad_first(coef_t.astype(bf16), hid_ref, gsend_a, gkeep_a, grec_a, ha)

    def s_ga2():
        state["ga2"] = grad_z(state["ga1"], gkeep_a, grec_a, zs_a, zrec_a)

    def s_a():
        ax.wait_recv()
        state["ap"] = go(remote(aoth.at[:, acols], aoth.at[:, acols], core))

    def s_low():
        local[3].wait()
        state["ap"].wait_recv()
        low_t = masked_pair(a_ref[0], aoth[...], hid_ref[...]).astype(bf16)
        state["gb1"] = grad_first(low_t, og_ref, gsend_b, gkeep_b, grec_b, hb)

    def s_gb2():
        state["gb2"] = grad_z(state["gb1"], gkeep_b, grec_b, zs_b, zrec_b)

    def s_ga3():
        state["ga3"] = grad_x(state["ga2"], zs_a, zrec_a, sum_a, xg_a, xgrec_a)

    def s_ga4():
        state["ga4"] = grad_y(state["ga3"], sum_a, xgrec_a, yg_a, ygrec_a)

    def s_gb3():
        state["gb3"] = grad_x(state["gb2"], zs_b, zrec_b, sum_b, xg_b, xgrec_b)

    def s_ga5():
        state["ga5"] = grad_gather(state["ga4"], yg_a, ygrec_a, full_a)

    def s_gb4():
        state["gb4"] = grad_y(state["gb3"], sum_b, xgrec_b, yg_b, ygrec_b)

    def s_gb5():
        state["gb5"] = grad_gather(state["gb4"], yg_b, ygrec_b, full_b)

    def s_ga6():
        state["ga6"] = grad_core(state["ga5"], full_a)

    def s_gb6():
        state["gb6"] = grad_core(state["gb5"], full_b)

    s_b()
    s_coef()

    for copy in ogc:
        copy.wait_recv()
    at = 0
    for yr in (0, 1):
        for cr in (0, 1):
            rows = []
            for ar in (0, 1):
                if yr or cr or ar:
                    rows.append(xrec[yr, cr, ar].astype(f32))
                else:
                    rows.append(og_ref[:, cols(f * slab, slab, slab)].astype(f32))
            pair = jnp.concatenate(rows, axis=0).astype(bf16)
            xs[at : at + 2 * toks] = pair
            at += 2 * toks

    adapter_steps = [
        [], [s_a], [s_low], [s_gb2], [], [s_ga3], [], [s_ga4, s_gb3], [s_gb4, s_ga5], [s_gb5],
        [s_ga6, s_gb6],
    ]
    lag = 5
    stage_matmul(0)
    s_ga2()
    for j in range(1, max(len(adapter_steps) + 1, chunks + lag)):
        if j < chunks:
            stage_matmul(j)
        if j <= chunks:
            stage_y(j - 1)
        if lag <= j < chunks + lag:
            stage_x(j - lag)
        if j - 1 < len(adapter_steps):
            for step in adapter_steps[j - 1]:
                step()
    for j in range(chunks):
        stage_out(j)
    grad_out(state["ga6"], full_a, ga_ref)
    grad_out(state["gb6"], full_b, gb_ref)
    for copy in started:
        copy.wait_send()
    for j in range(chunks):
        core_copy(j).wait_send()
        y_copy(j).wait_send()
        x_copy(j).wait_send()


def finish_kernel(scale, base_ref, fa_ref, fb_ref, out_ref, ga_ref, gb_ref):
    out_ref[...] = base_ref[...]
    for full, ref in ((fa_ref, ga_ref), (fb_ref, gb_ref)):
        halves, groups, _, width = full.shape
        for h in range(halves):
            for q in range(groups):
                at = (h * groups + q) * width
                ref[0, :, at : at + width] = scale * full[h, q].astype(jnp.float32)


def fused_on_device(
    adapter_index, output_gradient, hidden, frozen_down_weight, adapter_input_maps,
    adapter_output_maps,
):
    toks, model_width = output_gradient.shape
    hidden_width = hidden.shape[1]
    half, slab = frozen_down_weight.shape
    rank = adapter_input_maps.shape[1]
    groups = lax.axis_size("dp")
    devices = groups * lax.axis_size("adapter") * lax.axis_size("fsdp")
    scale = adapter_scale * lax.axis_size("adapter") / (toks * devices)
    chunks = chunk_count(half)
    ch = half // chunks
    f32, bf16 = jnp.float32, jnp.bfloat16

    def grad_scratch(width):
        wh = width // 2
        wq = wh // groups
        return [
            pltpu.VMEM((2 * rank, wh), bf16),
            pltpu.VMEM((2 * rank, wh), f32),
            pltpu.VMEM((2 * rank, wh), bf16),
            pltpu.VMEM((groups, 2 * rank, wq), bf16),
            pltpu.VMEM((groups - 1, 2 * rank, wq), bf16),
            pltpu.VMEM((rank, wq), f32),
            pltpu.VMEM((rank, wq), bf16),
            pltpu.VMEM((rank, wq), bf16),
            pltpu.VMEM((rank, wq), bf16),
            pltpu.VMEM((rank, wq), bf16),
            pltpu.VMEM((2, groups, rank, wq), bf16),
        ]

    copies = 4 + 7 + 2 * (3 + 2 * (groups - 1) + groups)
    vmem = pl.BlockSpec(memory_space=pltpu.VMEM)
    parts = pl.pallas_call(
        functools.partial(fused_kernel, chunks),
        out_shape=(
            jax.ShapeDtypeStruct((toks, hidden_width), bf16),
            jax.ShapeDtypeStruct((2, groups, rank, hidden_width // (2 * groups)), bf16),
            jax.ShapeDtypeStruct((2, groups, rank, model_width // (2 * groups)), bf16),
        ),
        in_specs=[vmem] + [pl.BlockSpec(memory_space=pltpu.HBM)] * 5,
        out_specs=(vmem, vmem, vmem),
        scratch_shapes=[
            pltpu.VMEM((toks, model_width), bf16),
            pltpu.VMEM((toks, hidden_width), bf16),
            pltpu.VMEM((1, rank, hidden_width), bf16),
            pltpu.VMEM((1, rank, model_width), bf16),
            pltpu.VMEM((chunks, ch, slab), bf16),
            pltpu.VMEM((2, 2, 2, toks, slab), bf16),
            pltpu.VMEM((8 * toks, slab), bf16),
            pltpu.VMEM((chunks, 2, 2 * toks, ch), f32),
            pltpu.VMEM((chunks, 2, 2 * toks, ch), bf16),
            pltpu.VMEM((chunks, 2, 2 * toks, ch), bf16),
            pltpu.VMEM((chunks, 2 * toks, ch), bf16),
            pltpu.VMEM((chunks, 2 * toks, ch), bf16),
            pltpu.VMEM((chunks, toks, ch), bf16),
            pltpu.VMEM((chunks, toks, ch), bf16),
            pltpu.VMEM((rank, hidden_width), bf16),
            pltpu.VMEM((rank, model_width), bf16),
            *grad_scratch(hidden_width),
            *grad_scratch(model_width),
            pltpu.SemaphoreType.DMA((4,)),
            pltpu.SemaphoreType.DMA((chunks,)),
            pltpu.SemaphoreType.DMA((copies,)),
            pltpu.SemaphoreType.DMA((copies,)),
            pltpu.SemaphoreType.DMA((3, chunks)),
            pltpu.SemaphoreType.DMA((3, chunks)),
        ],
        compiler_params=pltpu.CompilerParams(
            collective_id=0, has_side_effects=True, vmem_limit_bytes=64500000
        ),
    )(
        adapter_index.reshape(1, toks), output_gradient, hidden, frozen_down_weight,
        adapter_input_maps, adapter_output_maps,
    )
    return pl.pallas_call(
        functools.partial(finish_kernel, scale),
        out_shape=(
            jax.ShapeDtypeStruct((toks, hidden_width), bf16),
            jax.ShapeDtypeStruct((1, rank, hidden_width), f32),
            jax.ShapeDtypeStruct((1, rank, model_width), f32),
        ),
        in_specs=[vmem] * 3,
        out_specs=(vmem,) * 3,
        compiler_params=pltpu.CompilerParams(vmem_limit_bytes=64500000),
    )(*parts)


def per_device(mesh):
    def body(*args):
        fused = (
            mesh.shape["adapter"] == 2
            and mesh.shape["fsdp"] == 4
            and args[4].shape[0] == 1
        )
        return fused_on_device(*args) if fused else on_device(*args)

    return body


def solution(mesh):
    in_specs = (
        P(("dp", "adapter", "fsdp")),
        P(("dp", "adapter", "fsdp"), None),
        P(("dp", "adapter", "fsdp"), None),
        P("adapter", "fsdp"),
        P("adapter", None, None),
        P("adapter", None, None),
    )
    out_specs = (
        P(("dp", "adapter", "fsdp"), None),
        P("adapter", None, None),
        P("adapter", None, None),
    )
    return jax.shard_map(
        per_device(mesh), mesh=mesh, in_specs=in_specs, out_specs=out_specs, check_vma=False
    )
```
